32 devices in a mesh: ctx: 8 (over z, x), head: 4 (over y, core).
Axes of the slice: x: 2, y: 2, z: 4, core: 2. Of those that a mesh axis runs over, the one named last changes fastest.
Arguments:
- span_query: bfloat16 [2048, 16384], P('ctx', 'head'), may hold values from -5 to 5
- span_key: bfloat16 [2048, 1024], P('ctx', 'head'), may hold values from -12 to 12
- span_value: bfloat16 [2048, 1024], P('ctx', 'head'), may hold values from -6 to 6
- block_lists: int32 [16, 6], replicated, may hold values from 0 to 15, all different within a row
- owners: int32 [16], replicated, may hold values from 0 to 7, as said below
- cache_key: bfloat16 [32768, 1024], P('ctx', 'head'), may hold values from -12 to 12
- cache_value: bfloat16 [32768, 1024], P('ctx', 'head'), may hold values from -6 to 6
- sample_query: bfloat16 [64, 16384], P(None, 'head'), may hold values from -5 to 5
- sample_key: bfloat16 [64, 1024], P(None, 'head'), may hold values from -24 to 24
- sample_value: bfloat16 [64, 1024], P(None, 'head'), may hold values from -6 to 6
- out_weight: bfloat16 [16384, 16384], P('head', 'ctx'), may hold values from -0.046875 to 0.046875
Outputs:
- span_out: bfloat16 [2048, 16384], P('ctx', 'head')
- sample_out: bfloat16 [64, 16384], P(None, 'ctx')
- appended_key: bfloat16 [8192, 1024], P('ctx', 'head')
- appended_value: bfloat16 [8192, 1024], P('ctx', 'head')
The draws below stay inside these ranges and needn't reach their ends.
Inputs may be any that keep to these rules, and one draw needn't show every extreme that they name: `block_lists`: each row lists 6 different key blocks. `owners`: no owner has more than 8 blocks, and some owner has exactly 8.
All inputs are finite; a program needn't handle non-finite values.
Results may differ from the reference program's by a relative error of at most 0.00245.
The reference program's roundings to bfloat16 on the way count: a program that leaves them out, or rounds other values in their place, can miss the bound.
Values may be sent and summed in bfloat16 or wider, within the bound.
A program may use at most 128 MiB of HBM per device.

```python
import jax
import jax.numpy as jnp
from jax import lax

D = 16384
QH = 128
KVH = 8
HD = 128
BLOCK = 128
KSEL = 6
RES_DEV = 4096
SAMPLES = 64
QBLK = 2
MOST_BLOCKS = 8
SPAN = 2048
NBLK = 16
RESIDENT = 32768
N_CTX = 8


def draw_span_key(key, part):
    base = jnp.clip(jax.random.normal(jax.random.fold_in(key, 11), (SPAN, KVH * HD), jnp.float32) * 2.5, -12.0, 12.0)
    return base.astype(jnp.bfloat16)


def draw_span_query(key, part):
    base = jnp.clip(jax.random.normal(jax.random.fold_in(key, 13), (SPAN, QH * HD), jnp.float32), -5.0, 5.0)
    return base.astype(jnp.bfloat16)


def draw_cache_key(key, part):
    base = jnp.clip(jax.random.normal(jax.random.fold_in(key, 31), (RESIDENT, KVH * HD), jnp.float32) * 2.5, -12.0, 12.0)
    return base.astype(jnp.bfloat16)


def draw_sample_query(key, part):
    base = jnp.clip(jax.random.normal(jax.random.fold_in(key, 33), (SAMPLES, QH * HD), jnp.float32), -5.0, 5.0)
    return base.astype(jnp.bfloat16)


def draw_owners(key, part):
    owner_count = NBLK // QBLK
    slots = owner_count * MOST_BLOCKS
    favored = jax.random.randint(jax.random.fold_in(key, 21), (), 0, owner_count)
    order = jax.random.permutation(jax.random.fold_in(key, 22), slots).astype(jnp.int32)
    slot_ids = jnp.arange(slots, dtype=jnp.int32)
    ranking = order + jnp.where(slot_ids // MOST_BLOCKS == favored, 0, slots).astype(jnp.int32)
    picked = jnp.argsort(ranking, stable=True)[:NBLK].astype(jnp.int32)
    shuffle = jax.random.permutation(jax.random.fold_in(key, 23), NBLK)
    return (picked[shuffle] // MOST_BLOCKS).astype(jnp.int32)


def block_levels(own_key, dims, pieces, least, top_value):
    level, own = 1.0, jax.random.fold_in(own_key, 6)
    for axis_at, blocks in pieces:
        heights = jnp.exp(jax.random.uniform(jax.random.fold_in(own, axis_at), (blocks,), jnp.float32, least / len(pieces), top_value / len(pieces)))
        level = level * jnp.repeat(heights, dims[axis_at] // blocks).reshape([-1 if axis == axis_at else 1 for axis in range(len(dims))])
    return level


def picks_of(rng, rows, number_of, top, lift):
    sequence = jax.random.permutation(jax.random.fold_in(rng, 1), number_of)
    favour = sequence
    for power in range(3):
        favour = favour * favour // number_of
    favour = favour * lift // number_of
    lots = jax.random.randint(jax.random.fold_in(rng, 2), (rows, number_of), 0, 4096) + favour
    sure = jax.random.permutation(jax.random.fold_in(rng, 3), rows)[jnp.arange(number_of) % rows]
    lots = jnp.where(jnp.arange(rows)[:, None] == sure[None, :], 1 << 14, lots)
    priority = lots * number_of + jnp.arange(number_of)
    return lax.top_k(priority.astype(jnp.int32), top)[1].astype(jnp.int32)


def centred(stream_key, extent, spread, limit, cuts=(), kind=jnp.bfloat16):
    factor_of = block_levels(stream_key, extent, cuts, -0.22, 0.18) if cuts else 1.0
    values = jax.random.normal(stream_key, extent, jnp.float32) * spread * factor_of
    return jnp.minimum(jnp.maximum(values, -limit), limit).astype(kind)


def setup_inputs(seed: int = 0) -> dict:
    key_of = jax.random.split(jax.random.key(seed), 12)
    span_query = draw_span_query(jax.random.fold_in(key_of[11], 71), 0)
    span_key = draw_span_key(jax.random.fold_in(key_of[11], 71), 0)
    span_value = centred(key_of[2], (SPAN, KVH * HD), 1.0, 6.0, ((0, 8), (1, 4)))
    block_lists = picks_of(key_of[3], NBLK, NBLK, KSEL, 6144)
    owners = draw_owners(jax.random.fold_in(key_of[11], 71), 0)
    cache_key = draw_cache_key(jax.random.fold_in(key_of[11], 71), 0)
    cache_value = centred(key_of[6], (RESIDENT, KVH * HD), 1.0, 6.0, ((0, 8), (1, 4)))
    sample_query = draw_sample_query(jax.random.fold_in(key_of[11], 71), 0)
    sample_key = centred(key_of[8], (SAMPLES, KVH * HD), 4.0, 24.0, ((1, 4),))
    sample_value = centred(key_of[9], (SAMPLES, KVH * HD), 1.0, 6.0, ((1, 4),))
    out_weight = centred(key_of[10], (QH * HD, D), (QH * HD) ** -0.5, 0.046875, ((0, 4), (1, 8)))
    return {"span_query": span_query, "span_key": span_key, "span_value": span_value, "block_lists": block_lists, "owners": owners, "cache_key": cache_key, "cache_value": cache_value, "sample_query": sample_query, "sample_key": sample_key, "sample_value": sample_value, "out_weight": out_weight}


NEG = -1.0e30


def reference(span_query, span_key, span_value, block_lists, owners, cache_key, cache_value, sample_query, sample_key, sample_value, out_weight):
    scale = HD ** -0.5
    group = QH // KVH
    key_blocks = span_key.reshape(NBLK, BLOCK, KVH, HD)
    value_blocks = span_value.reshape(NBLK, BLOCK, KVH, HD)
    query_blocks = span_query.reshape(NBLK, BLOCK, KVH, group, HD)
    width = (KSEL + 1) * BLOCK
    column = jnp.arange(width, dtype=jnp.int32)
    which = column // BLOCK
    within = column % BLOCK
    row_ids = jnp.arange(BLOCK, dtype=jnp.int32)

    def one_block(index):
        chosen = jnp.concatenate([index[None], block_lists[index]]).astype(jnp.int32)
        keys = key_blocks[chosen].reshape(width, KVH, HD).astype(jnp.float32)
        values = value_blocks[chosen].reshape(width, KVH, HD).astype(jnp.float32)
        queries = query_blocks[index].astype(jnp.float32)
        scores = jnp.einsum("qkgd,nkd->kgqn", queries, keys) * scale
        allowed = jnp.where(which[None, :] == 0, within[None, :] <= row_ids[:, None], (chosen[which] != index)[None, :])
        scores = jnp.where(allowed, scores, NEG)
        peak = jnp.max(scores, axis=-1, keepdims=True)
        weights = jnp.exp(scores - peak)
        probs = (weights / jnp.sum(weights, axis=-1, keepdims=True)).astype(jnp.bfloat16)
        probs = lax.optimization_barrier(probs).astype(jnp.float32)
        out = jnp.einsum("kgqn,nkd->qkgd", probs, values)
        return out.astype(jnp.bfloat16).reshape(BLOCK, QH * HD)

    span_out = lax.map(one_block, jnp.arange(NBLK, dtype=jnp.int32)).reshape(NBLK * BLOCK, QH * HD)

    owner_ids = jnp.arange(N_CTX, dtype=jnp.int32)
    mine = (owners[None, :] == owner_ids[:, None]).astype(jnp.int32)
    rank = (jnp.cumsum(mine, axis=1) - 1).astype(jnp.int32)
    slot_ids = jnp.arange(MOST_BLOCKS, dtype=jnp.int32)
    hits = (mine[:, None, :] == 1) & (rank[:, None, :] == slot_ids[None, :, None])
    picked = jnp.sum(jnp.where(hits, jnp.arange(NBLK, dtype=jnp.int32)[None, None, :], 0), axis=-1).astype(jnp.int32)
    live = jnp.any(hits, axis=-1)
    flat_keys = span_key.reshape(NBLK, BLOCK, KVH * HD)
    flat_values = span_value.reshape(NBLK, BLOCK, KVH * HD)
    appended_key = jnp.where(live[:, :, None, None], flat_keys[picked], jnp.zeros((), jnp.bfloat16)).reshape(N_CTX * MOST_BLOCKS * BLOCK, KVH * HD)
    appended_value = jnp.where(live[:, :, None, None], flat_values[picked], jnp.zeros((), jnp.bfloat16)).reshape(N_CTX * MOST_BLOCKS * BLOCK, KVH * HD)

    samples = sample_query.reshape(SAMPLES, KVH, group, HD).astype(jnp.float32)

    def group_partial(pair):
        keys, values = pair
        scores = jnp.einsum("skgd,nkd->kgsn", samples, keys.astype(jnp.float32)) * scale
        peak = jnp.max(scores, axis=-1)
        weights = jnp.exp(scores - peak[..., None])
        total = jnp.sum(weights, axis=-1)
        rounded = lax.optimization_barrier(weights.astype(jnp.bfloat16)).astype(jnp.float32)
        summed = jnp.einsum("kgsn,nkd->kgsd", rounded, values.astype(jnp.float32))
        return peak, total, summed

    res_peak, res_total, res_sum = lax.map(group_partial, (cache_key.reshape(N_CTX, RES_DEV, KVH, HD), cache_value.reshape(N_CTX, RES_DEV, KVH, HD)))
    blk_peak, blk_total, blk_sum = lax.map(group_partial, (key_blocks, value_blocks))
    peaks = jnp.concatenate([res_peak, blk_peak], axis=0)
    totals = jnp.concatenate([res_total, blk_total], axis=0)
    sums = jnp.concatenate([res_sum, blk_sum], axis=0)
    own_keys = sample_key.reshape(SAMPLES, KVH, HD).astype(jnp.float32)
    own_score = jnp.einsum("skgd,skd->kgs", samples, own_keys) * scale
    top = jnp.maximum(jnp.max(peaks, axis=0), own_score)
    factor = jnp.exp(peaks - top[None])
    own_factor = jnp.exp(own_score - top)
    total = jnp.sum(factor * totals, axis=0) + own_factor
    own_values = jnp.transpose(sample_value.reshape(SAMPLES, KVH, HD).astype(jnp.float32), (1, 0, 2))[:, None, :, :]
    combined = jnp.sum(factor[..., None] * sums, axis=0) + own_factor[..., None] * own_values
    attended = (combined / total[..., None]).astype(jnp.bfloat16)
    attended = jnp.transpose(attended, (2, 0, 1, 3)).reshape(SAMPLES, QH * HD)
    sample_out = jnp.dot(attended, out_weight, preferred_element_type=jnp.float32).astype(jnp.bfloat16)
    return span_out, sample_out, appended_key, appended_value
```

```python
import functools

import jax
import jax.numpy as jnp
from jax import lax
from jax.experimental import pallas as pl
from jax.experimental.pallas import tpu as pltpu
from jax.sharding import PartitionSpec as P

HD = 128
BLOCK = 128
MOST_BLOCKS = 8
NEG = -1e30
SCALE = HD ** -0.5
EXP2_SCALE = SCALE * 1.4426950408889634


def dot_t(a, b):
    return lax.dot_general(a, b, (((1,), (1,)), ((), ())), preferred_element_type=jnp.float32)


def dot(a, b):
    return jnp.dot(a, b, preferred_element_type=jnp.float32)


def lane_fold(op, x):
    parts = [x[:, i * 128 : (i + 1) * 128] for i in range(x.shape[1] // 128)]
    while len(parts) > 1:
        parts = [op(*parts[i : i + 2]) if i + 1 < len(parts) else parts[i] for i in range(0, len(parts), 2)]
    return parts[0]


def column(ref, head, start, size):
    return ref[pl.ds(start, size), pl.ds(pl.multiple_of(head * HD, HD), HD)]


def decode_tile(dims, tile, q_ref, ck_ref, cv_ref, sk_ref, sv_ref, s_ref):
    samples, group, per, chunk = dims
    rows = per * samples
    head = (tile * per) // group
    q = jnp.concatenate([column(q_ref, tile * per + g, 0, samples) for g in range(per)], axis=0)
    resident = ck_ref.shape[0]
    high = jnp.full((rows, 128), NEG, jnp.float32)
    for c in range(resident // chunk):
        s = dot_t(q, column(ck_ref, head, c * chunk, chunk))
        s_ref[:, c * chunk : (c + 1) * chunk] = s
        high = jnp.maximum(high, lane_fold(jnp.maximum, s))
    peak = jnp.max(high, axis=1, keepdims=True)
    total = jnp.zeros((rows, 128), jnp.float32)
    acc = jnp.zeros((rows, HD), jnp.float32)
    for c in range(resident // chunk):
        w = jnp.exp2((s_ref[:, c * chunk : (c + 1) * chunk] - peak) * EXP2_SCALE)
        total = total + lane_fold(jnp.add, w)
        acc = acc + dot(w.astype(jnp.bfloat16), column(cv_ref, head, c * chunk, chunk))
    groups = [(peak, jnp.sum(total, axis=1, keepdims=True), acc)]
    for b in range(sk_ref.shape[0] // BLOCK):
        s = dot_t(q, column(sk_ref, head, b * BLOCK, BLOCK))
        top = jnp.max(s, axis=1, keepdims=True)
        w = jnp.exp2((s - top) * EXP2_SCALE)
        part = dot(w.astype(jnp.bfloat16), column(sv_ref, head, b * BLOCK, BLOCK))
        groups.append((top, jnp.sum(w, axis=1, keepdims=True), part))
    top = functools.reduce(jnp.maximum, [g[0] for g in groups])
    factors = [jnp.exp2((g[0] - top) * EXP2_SCALE) for g in groups]
    total = sum(f * g[1] for f, g in zip(factors, groups))
    acc = sum(f * g[2] for f, g in zip(factors, groups))
    return top, total, acc


def prefill_heads(heads, block, first_head, q_ref, keys, values, flags, causal, out_ref):
    for g in range(heads):
        q = column(q_ref, first_head + g, block * BLOCK, BLOCK)
        s = dot_t(q, keys)
        parts = [s[:, :BLOCK] + causal]
        for i, flag in enumerate(flags):
            parts.append(s[:, (i + 1) * BLOCK : (i + 2) * BLOCK] + flag)
        s = jnp.concatenate(parts, axis=1)
        peak = jnp.max(lane_fold(jnp.maximum, s), axis=1, keepdims=True)
        w = jnp.exp2((s - peak) * EXP2_SCALE)
        inverse = 1.0 / jnp.sum(lane_fold(jnp.add, w), axis=1, keepdims=True)
        probs = (w * inverse).astype(jnp.bfloat16)
        out_ref[pl.ds(block * BLOCK, BLOCK), pl.ds(pl.multiple_of((first_head + g) * HD, HD), HD)] = dot(
            probs, values
        ).astype(jnp.bfloat16)


def prefill_all(dims, position, lists_ref, q_ref, kg_ref, vg_ref, kc_ref, vc_ref, out_ref, between=None):
    qblk, kvh, group, ksel, heads = dims
    causal = jnp.where(
        lax.broadcasted_iota(jnp.int32, (BLOCK, BLOCK), 1) <= lax.broadcasted_iota(jnp.int32, (BLOCK, BLOCK), 0),
        0.0,
        NEG,
    ).astype(jnp.float32)
    for b in range(qblk):
        own = position * qblk + b
        kc_ref[:BLOCK, :] = kg_ref[own]
        vc_ref[:BLOCK, :] = vg_ref[own]
        flags = []
        for i in range(ksel):
            listed = lists_ref[own, i]
            kc_ref[(i + 1) * BLOCK : (i + 2) * BLOCK, :] = kg_ref[listed]
            vc_ref[(i + 1) * BLOCK : (i + 2) * BLOCK, :] = vg_ref[listed]
            flags.append(jnp.where(listed == own, NEG, 0.0).astype(jnp.float32))
        for k in range(kvh):

            def step(i, carry, b=b, k=k, flags=flags):
                prefill_heads(
                    heads,
                    b,
                    k * group + i * heads,
                    q_ref,
                    kc_ref[:, k * HD : (k + 1) * HD],
                    vc_ref[:, k * HD : (k + 1) * HD],
                    flags,
                    causal,
                    out_ref,
                )
                return carry

            lax.fori_loop(0, group // heads, step, 0)
            if between is not None:
                between(b * kvh + k)


def append_all(position, owners_ref, kg_ref, vg_ref, ak_ref, av_ref):
    blocks = kg_ref.shape[0]

    def count(b, carry):
        rank, picked = carry
        mine = owners_ref[b] == position
        picked = tuple(jnp.where(mine & (rank == slot), b, p) for slot, p in enumerate(picked))
        return rank + mine.astype(jnp.int32), picked

    rank, picked = lax.fori_loop(
        0, blocks, count, (jnp.int32(0), tuple(jnp.int32(0) for _ in range(MOST_BLOCKS)))
    )
    for slot in range(MOST_BLOCKS):
        live = jnp.broadcast_to(rank, (BLOCK, kg_ref.shape[2])) > slot
        rows = slice(slot * BLOCK, (slot + 1) * BLOCK)
        for src, dst in ((kg_ref, ak_ref), (vg_ref, av_ref)):
            x = src[picked[slot]].astype(jnp.float32)
            dst[rows, :] = jnp.where(live, x, 0.0).astype(jnp.bfloat16)


def decode_kernel(dims, tiles, q_ref, ck_ref, cv_ref, sk_ref, sv_ref, m_ref, l_ref, acc_ref, s_ref):
    samples, _, per, _ = dims

    def step(tile, carry):
        m, l, acc = decode_tile(dims, tile, q_ref, ck_ref, cv_ref, sk_ref, sv_ref, s_ref)
        m_ref[tile] = jnp.broadcast_to(m, acc.shape)
        l_ref[tile] = jnp.broadcast_to(l, acc.shape)
        acc_ref[tile] = acc
        return carry

    lax.fori_loop(0, tiles, step, 0)


def prefill_kernel(dims, lists_ref, owners_ref, q_ref, kg_ref, vg_ref, out_ref, ak_ref, av_ref, kc_ref, vc_ref):
    position = lax.axis_index("ctx")
    append_all(position, owners_ref, kg_ref, vg_ref, ak_ref, av_ref)
    prefill_all(dims, position, lists_ref, q_ref, kg_ref, vg_ref, kc_ref, vc_ref, out_ref)


VM = pl.BlockSpec(memory_space=pltpu.VMEM)
SM = pl.BlockSpec(memory_space=pltpu.SMEM)


def local(n_ctx, span_query, span_key, span_value, block_lists, owners, cache_key, cache_value, sample_query, sample_key, sample_value, out_weight):
    tokens = span_query.shape[0]
    kvh = span_key.shape[1] // HD
    group = span_query.shape[1] // HD // kvh
    qblk = tokens // BLOCK
    samples = sample_query.shape[0]
    per = kvh * group // n_ctx
    resident = cache_key.shape[0]
    kg = lax.all_gather(span_key, "ctx", axis=0, tiled=True).reshape(-1, BLOCK, kvh * HD)
    vg = lax.all_gather(span_value, "ctx", axis=0, tiled=True).reshape(-1, BLOCK, kvh * HD)
    dims = (samples, group, per, 512)
    f32 = jax.ShapeDtypeStruct((n_ctx, per * samples, HD), jnp.float32)
    m, l, acc = pl.pallas_call(
        functools.partial(decode_kernel, dims, n_ctx),
        out_shape=(f32, f32, f32),
        in_specs=[VM] * 5,
        out_specs=(VM,) * 3,
        scratch_shapes=[pltpu.VMEM((per * samples, resident), jnp.float32)],
        compiler_params=pltpu.CompilerParams(vmem_limit_bytes=60 << 20),
        cost_estimate=pl.CostEstimate(flops=5 << 30, bytes_accessed=8 << 20, transcendentals=9 << 20),
        name="decode",
    )(sample_query, cache_key, cache_value, span_key, span_value)
    width = (block_lists.shape[1] + 1) * BLOCK
    slots = jax.ShapeDtypeStruct((MOST_BLOCKS * BLOCK, kvh * HD), jnp.bfloat16)
    span_out, appended_key, appended_value = pl.pallas_call(
        functools.partial(prefill_kernel, (qblk, kvh, group, block_lists.shape[1], 4)),
        out_shape=(jax.ShapeDtypeStruct(span_query.shape, jnp.bfloat16), slots, slots),
        in_specs=[SM, SM, VM, VM, VM],
        out_specs=(VM,) * 3,
        scratch_shapes=[pltpu.VMEM((width, kvh * HD), jnp.bfloat16)] * 2,
        compiler_params=pltpu.CompilerParams(vmem_limit_bytes=60 << 20),
        cost_estimate=pl.CostEstimate(flops=4 << 30, bytes_accessed=8 << 20, transcendentals=7 << 20),
        name="prefill",
    )(block_lists, owners, span_query, kg, vg)
    m, l = m[:, :, :1] * SCALE, l[:, :, :1]
    top = lax.pmax(m, "ctx")
    factor = jnp.exp(m - top)
    l, acc = lax.psum((l * factor, acc * factor), "ctx")
    shape = (kvh, group, samples, -1)
    top, l, acc = top.reshape(shape), l.reshape(shape), acc.reshape(shape)
    asked = sample_query.reshape(samples, kvh, group, HD)
    own_keys = sample_key.reshape(samples, kvh, HD)
    own = jnp.einsum("skgd,skd->kgs", asked, own_keys, preferred_element_type=jnp.float32)[..., None] * SCALE
    own_values = jnp.transpose(sample_value.reshape(samples, kvh, HD).astype(jnp.float32), (1, 0, 2))[:, None]
    final = jnp.maximum(top, own)
    old, new = jnp.exp(top - final), jnp.exp(own - final)
    attended = ((acc * old + new * own_values) / (l * old + new)).astype(jnp.bfloat16)
    attended = jnp.transpose(attended, (2, 0, 1, 3)).reshape(samples, -1)
    partial_out = jnp.dot(attended, out_weight, preferred_element_type=jnp.float32)
    sample_out = lax.psum(partial_out, "head").astype(jnp.bfloat16)
    return span_out, sample_out, appended_key, appended_value


def solution(mesh):
    c = P("ctx", "head")
    return jax.shard_map(
        functools.partial(local, mesh.shape["ctx"]),
        mesh=mesh,
        in_specs=(c, c, c, P(), P(), c, c, P(None, "head"), P(None, "head"), P(None, "head"), P("head", "ctx")),
        out_specs=(c, P(None, "ctx"), c, c),
        check_vma=False,
    )
```

```python
import functools

import jax
import jax.numpy as jnp
from jax import lax
from jax.experimental import pallas as pl
from jax.experimental.pallas import tpu as pltpu
from jax.sharding import PartitionSpec as P

HD = 128
BLOCK = 128
MOST_BLOCKS = 8
NEG = -1e30
SCALE = HD ** -0.5
EXP2_SCALE = SCALE * 1.4426950408889634


def dot_t(a, b):
    return lax.dot_general(a, b, (((1,), (1,)), ((), ())), preferred_element_type=jnp.float32)


def dot(a, b):
    return jnp.dot(a, b, preferred_element_type=jnp.float32)


def lane_fold(op, x):
    parts = [x[:, i * 128 : (i + 1) * 128] for i in range(x.shape[1] // 128)]
    while len(parts) > 1:
        parts = [op(*parts[i : i + 2]) if i + 1 < len(parts) else parts[i] for i in range(0, len(parts), 2)]
    return parts[0]


def column(ref, head, start, size):
    return ref[pl.ds(start, size), pl.ds(pl.multiple_of(head * HD, HD), HD)]


def decode_tile(dims, tile, q_ref, ck_ref, cv_ref, sk_ref, sv_ref, s_ref):
    samples, group, per, chunk = dims
    rows = per * samples
    head = lax.div(tile * per, group)
    q = jnp.concatenate([column(q_ref, tile * per + g, 0, samples) for g in range(per)], axis=0)
    resident = ck_ref.shape[0]
    high = jnp.full((rows, 128), NEG, jnp.float32)
    for c in range(resident // chunk):
        s = dot_t(q, column(ck_ref, head, c * chunk, chunk))
        s_ref[:, c * chunk : (c + 1) * chunk] = s
        high = jnp.maximum(high, lane_fold(jnp.maximum, s))
    peak = jnp.max(high, axis=1, keepdims=True)
    total = jnp.zeros((rows, 128), jnp.float32)
    acc = jnp.zeros((rows, HD), jnp.float32)
    for c in range(resident // chunk):
        w = jnp.exp2((s_ref[:, c * chunk : (c + 1) * chunk] - peak) * EXP2_SCALE)
        total = total + lane_fold(jnp.add, w)
        acc = acc + dot(w.astype(jnp.bfloat16), column(cv_ref, head, c * chunk, chunk))
    groups = [(peak, jnp.sum(total, axis=1, keepdims=True), acc)]
    for b in range(sk_ref.shape[0] // BLOCK):
        s = dot_t(q, column(sk_ref, head, b * BLOCK, BLOCK))
        top = jnp.max(s, axis=1, keepdims=True)
        w = jnp.exp2((s - top) * EXP2_SCALE)
        part = dot(w.astype(jnp.bfloat16), column(sv_ref, head, b * BLOCK, BLOCK))
        groups.append((top, jnp.sum(w, axis=1, keepdims=True), part))
    top = functools.reduce(jnp.maximum, [g[0] for g in groups])
    factors = [jnp.exp2((g[0] - top) * EXP2_SCALE) for g in groups]
    total = sum(f * g[1] for f, g in zip(factors, groups))
    acc = sum(f * g[2] for f, g in zip(factors, groups))
    return top, total, acc


def prefill_heads(heads, block, first_head, q_ref, keys, values, flags, causal, out_ref):
    for g in range(heads):
        q = column(q_ref, first_head + g, block * BLOCK, BLOCK)
        s = dot_t(q, keys)
        parts = [s[:, :BLOCK] + causal]
        for i, flag in enumerate(flags):
            parts.append(s[:, (i + 1) * BLOCK : (i + 2) * BLOCK] + flag)
        s = jnp.concatenate(parts, axis=1)
        peak = jnp.max(lane_fold(jnp.maximum, s), axis=1, keepdims=True)
        w = jnp.exp2((s - peak) * EXP2_SCALE)
        inverse = 1.0 / jnp.sum(lane_fold(jnp.add, w), axis=1, keepdims=True)
        probs = (w * inverse).astype(jnp.bfloat16)
        out_ref[pl.ds(block * BLOCK, BLOCK), pl.ds(pl.multiple_of((first_head + g) * HD, HD), HD)] = dot(
            probs, values
        ).astype(jnp.bfloat16)


def prefill_all(dims, position, lists_ref, q_ref, kg_ref, vg_ref, kc_ref, vc_ref, out_ref, between=None):
    qblk, kvh, group, ksel, heads = dims
    causal = jnp.where(
        lax.broadcasted_iota(jnp.int32, (BLOCK, BLOCK), 1) <= lax.broadcasted_iota(jnp.int32, (BLOCK, BLOCK), 0),
        0.0,
        NEG,
    ).astype(jnp.float32)
    for b in range(qblk):
        own = position * qblk + b
        kc_ref[:BLOCK, :] = kg_ref[own]
        vc_ref[:BLOCK, :] = vg_ref[own]
        flags = []
        for i in range(ksel):
            listed = lists_ref[own, i]
            kc_ref[(i + 1) * BLOCK : (i + 2) * BLOCK, :] = kg_ref[listed]
            vc_ref[(i + 1) * BLOCK : (i + 2) * BLOCK, :] = vg_ref[listed]
            flags.append(jnp.where(listed == own, NEG, 0.0).astype(jnp.float32))
        for k in range(kvh):

            def step(i, carry, b=b, k=k, flags=flags):
                prefill_heads(
                    heads,
                    b,
                    k * group + i * heads,
                    q_ref,
                    kc_ref[:, k * HD : (k + 1) * HD],
                    vc_ref[:, k * HD : (k + 1) * HD],
                    flags,
                    causal,
                    out_ref,
                )
                return carry

            lax.fori_loop(0, group // heads, step, 0)
            if between is not None:
                between(b * kvh + k)


def append_all(position, owners_ref, kg_ref, vg_ref, ak_ref, av_ref):
    blocks = kg_ref.shape[0]

    def count(b, carry):
        rank, picked = carry
        mine = owners_ref[b] == position
        picked = tuple(jnp.where(mine & (rank == slot), b, p) for slot, p in enumerate(picked))
        return rank + mine.astype(jnp.int32), picked

    rank, picked = lax.fori_loop(
        0, blocks, count, (jnp.int32(0), tuple(jnp.int32(0) for _ in range(MOST_BLOCKS)))
    )
    for slot in range(MOST_BLOCKS):
        live = jnp.broadcast_to(rank, (BLOCK, kg_ref.shape[2])) > slot
        rows = slice(slot * BLOCK, (slot + 1) * BLOCK)
        for src, dst in ((kg_ref, ak_ref), (vg_ref, av_ref)):
            x = src[picked[slot]].astype(jnp.float32)
            dst[rows, :] = jnp.where(live, x, 0.0).astype(jnp.bfloat16)


MESH = pl.DeviceIdType.MESH


def pack_stats(m, l, rows):
    lane = lax.broadcasted_iota(jnp.int32, (rows, 128), 1)
    both = jnp.where(lane < 4, jnp.broadcast_to(m, (rows, 128)), jnp.broadcast_to(l, (rows, 128)))
    if rows < 128:
        both = jnp.concatenate([both] * (128 // rows), axis=0)
    slabs = [both[i * 128 : (i + 1) * 128].T[:8] for i in range(max(1, rows // 128))]
    return jnp.concatenate(slabs, axis=0)


def unpack_stats(slabs, rows):
    spread = [
        jnp.concatenate([slabs[i * 8 : (i + 1) * 8]] * 16, axis=0).T for i in range(max(1, rows // 128))
    ]
    spread = jnp.concatenate(spread, axis=0)[:rows]
    return spread[:, 0:1], spread[:, 4:5]


def layer_kernel(
    n_ctx,
    n_head,
    dims,
    pre_dims,
    lists_ref,
    owners_ref,
    q_ref,
    sk_ref,
    sv_ref,
    sk_ref_own,
    sv_ref_own,
    span_k,
    span_v,
    ck_hbm,
    cv_hbm,
    sq_hbm,
    w_hbm,
    out_ref,
    sample_ref,
    ak_ref,
    av_ref,
    ck,
    cv,
    sq,
    w,
    kg,
    vg,
    s_ref,
    kc,
    vc,
    part,
    took,
    att,
    hpart,
    htook,
    hout,
    in_sem,
    g_send,
    g_recv,
    p_send,
    p_recv,
    a_send,
    a_recv,
    h_send,
    h_recv,
    o_send,
    o_recv,
):
    samples, group, per, _ = dims
    rows = per * samples
    me = lax.axis_index("ctx")
    hme = lax.axis_index("head")
    qblk = span_k.shape[0]
    n_hi = n_ctx // 2
    hi, lo = lax.div(me, 2), lax.rem(me, 2)

    def ctx(j):
        return lax.rem(me + j + n_ctx, n_ctx)

    def head(j):
        return lax.rem(hme + j + n_head, n_head)

    pair = hi * 2 + 1 - lo

    local_copies = [
        pltpu.make_async_copy(a, b, in_sem.at[i])
        for i, (a, b) in enumerate(
            (
                (ck_hbm, ck),
                (cv_hbm, cv),
                (sq_hbm, sq),
                (w_hbm, w),
                (span_k, kg.at[pl.ds(me * qblk, qblk)]),
                (span_v, vg.at[pl.ds(me * qblk, qblk)]),
            )
        )
    ]
    for i in (4, 5, 0, 1, 2, 3):
        local_copies[i].start()
    for i in (4, 5):
        local_copies[i].wait()

    barrier = pltpu.get_barrier_semaphore()
    for j in range(1, n_ctx):
        pl.semaphore_signal(barrier, inc=1, device_id={"ctx": ctx(j)}, device_id_type=MESH)
    for j in range(1, n_head):
        pl.semaphore_signal(barrier, inc=1, device_id={"head": head(j)}, device_id_type=MESH)
    pl.semaphore_wait(barrier, n_ctx - 1 + n_head - 1)

    def gather_copy(kind, index, src, owner, target):
        full = (kg, vg)[kind]
        view = full.at[pl.ds(owner * qblk, qblk)]
        return pltpu.make_async_remote_copy(
            src_ref=view if src is None else src,
            dst_ref=view,
            send_sem=g_send.at[kind, index],
            recv_sem=g_recv.at[kind, index],
            device_id={"ctx": target},
            device_id_type=MESH,
        )

    for h in range(1, n_hi):
        for kind, src in enumerate((span_k, span_v)):
            gather_copy(kind, h, src, me, lax.rem(hi + h, n_hi) * 2 + lo).start()
    for kind, src in enumerate((span_k, span_v)):
        gather_copy(kind, 0, src, me, pair).start()

    def forward(h):
        owner = lax.rem(hi - h + n_hi, n_hi) * 2 + lo
        for kind in range(2):
            gather_copy(kind, h, None, owner, pair).wait_recv()
        for kind in range(2):
            gather_copy(kind, n_hi + h, None, owner, pair).start()

    def part_copy(j):
        return pltpu.make_async_remote_copy(
            src_ref=part.at[j],
            dst_ref=took.at[j],
            send_sem=p_send.at[j],
            recv_sem=p_recv.at[j],
            device_id={"ctx": ctx(j)},
            device_id_type=MESH,
        )

    for i in (0, 1):
        local_copies[i].wait()

    def one_tile(j):
        m, l, acc = decode_tile(dims, ctx(j), q_ref, ck, cv, sk_ref, sv_ref, s_ref)
        part[j, :rows, :] = acc
        part[j, rows:, :] = pack_stats(m, l, rows)

    def tile_step(j, carry):
        one_tile(j)
        part_copy(j).start()
        return carry

    points = min(3, n_hi - 1)
    first, sent = 1, 1
    for point in range(points):
        last = n_ctx * (point + 2) // (points + 1)
        lax.fori_loop(first, min(last, n_ctx), tile_step, 0)
        first = min(last, n_ctx)
        if point == points - 1:
            lax.fori_loop(first, n_ctx, tile_step, 0)
            one_tile(0)
        until = 1 + (n_hi - 1) * (point + 1) // points
        for h in range(sent, until):
            forward(h)
        sent = until

    for i in (2,):
        local_copies[i].wait()
    for kind in range(2):
        gather_copy(kind, 0, None, pair, pair).wait_recv()
    for h in range(1, n_hi):
        owner = lax.rem(hi - h + n_hi, n_hi) * 2 + 1 - lo
        for kind in range(2):
            gather_copy(kind, n_hi + h, None, owner, pair).wait_recv()

    def att_copy(j):
        return pltpu.make_async_remote_copy(
            src_ref=att.at[0],
            dst_ref=att.at[j],
            send_sem=a_send.at[j],
            recv_sem=a_recv.at[j],
            device_id={"ctx": ctx(j)},
            device_id_type=MESH,
        )

    def combine():
        key_head = lax.div(me * per, group)
        own_key = column(sk_ref_own, key_head, 0, samples).astype(jnp.float32)
        own_value = column(sv_ref_own, key_head, 0, samples).astype(jnp.float32)
        own = jnp.concatenate(
            [
                jnp.sum(
                    column(q_ref, me * per + g, 0, samples).astype(jnp.float32) * own_key, axis=1, keepdims=True
                )
                for g in range(per)
            ],
            axis=0,
        )
        for j in range(1, n_ctx):
            part_copy(j).wait_recv()
        stats = [unpack_stats((took if j else part)[j, rows:, :], rows) for j in range(n_ctx)]
        top = functools.reduce(jnp.maximum, [s[0] for s in stats] + [own])
        new = jnp.exp2((own - top) * EXP2_SCALE)
        total = new
        acc = new * jnp.concatenate([own_value] * per, axis=0)
        for j in range(n_ctx):
            factor = jnp.exp2((stats[j][0] - top) * EXP2_SCALE)
            total = total + factor * stats[j][1]
            acc = acc + factor * (took if j else part)[j, :rows, :]
        attended = (acc / total).astype(jnp.bfloat16)
        for g in range(per):
            att[0, :, g * HD : (g + 1) * HD] = attended[g * samples : (g + 1) * samples]
        for j in range(1, n_ctx):
            att_copy(j).start()

    columns = w.shape[1] // n_head
    depth = per * HD

    def head_copy(j):
        return pltpu.make_async_remote_copy(
            src_ref=hpart.at[j],
            dst_ref=htook.at[j],
            send_sem=h_send.at[j],
            recv_sem=h_recv.at[j],
            device_id={"head": head(j)},
            device_id_type=MESH,
        )

    def project():
        for j in range(1, n_ctx):
            att_copy(j).wait_recv()
        local_copies[3].wait()
        for j in [*range(1, n_head), 0]:
            where = pl.ds(pl.multiple_of(head(j) * columns, 128), columns)
            total = jnp.zeros((samples, columns), jnp.float32)
            for c in range(n_ctx):
                total = total + dot(att[c], w[pl.ds(pl.multiple_of(ctx(-c) * depth, 128), depth), where])
            hpart[j] = total
            if j:
                head_copy(j).start()

    def out_copy(j):
        return pltpu.make_async_remote_copy(
            src_ref=hout.at[0],
            dst_ref=hout.at[j],
            send_sem=o_send.at[j],
            recv_sem=o_recv.at[j],
            device_id={"head": head(j)},
            device_id_type=MESH,
        )

    def between(unit):
        if unit == COMBINE_AFTER:
            combine()
        if unit == PROJECT_AFTER:
            project()

    prefill_all(pre_dims, me, lists_ref, sq, kg, vg, kc, vc, out_ref, between)
    for j in range(1, n_head):
        head_copy(j).wait_recv()
    total = hpart[0]
    for j in range(1, n_head):
        total = total + htook[j]
    hout[0] = total.astype(jnp.bfloat16)
    for j in range(1, n_head):
        out_copy(j).start()
    append_all(me, owners_ref, kg, vg, ak_ref, av_ref)
    for j in range(1, n_head):
        out_copy(j).wait_recv()
    for j in range(n_head):
        sample_ref[:, pl.ds(pl.multiple_of(head(-j) * columns, 128), columns)] = hout[j]

    for kind, src in enumerate((span_k, span_v)):
        for h in range(n_hi):
            gather_copy(kind, h, src, me, pair).wait_send()
        for h in range(1, n_hi):
            gather_copy(kind, n_hi + h, None, me, pair).wait_send()
    for j in range(1, n_ctx):
        part_copy(j).wait_send()
        att_copy(j).wait_send()
    for j in range(1, n_head):
        head_copy(j).wait_send()
        out_copy(j).wait_send()


VM = pl.BlockSpec(memory_space=pltpu.VMEM)
SM = pl.BlockSpec(memory_space=pltpu.SMEM)
ANY = pl.BlockSpec(memory_space=pl.ANY)
COMBINE_AFTER = 1
PROJECT_AFTER = 3


def local(n_ctx, n_head, span_query, span_key, span_value, block_lists, owners, cache_key, cache_value, sample_query, sample_key, sample_value, out_weight):
    tokens = span_query.shape[0]
    kvh = span_key.shape[1] // HD
    group = span_query.shape[1] // HD // kvh
    qblk = tokens // BLOCK
    samples = sample_query.shape[0]
    per = kvh * group // n_ctx
    rows = per * samples
    resident = cache_key.shape[0]
    ksel = block_lists.shape[1]
    width = (ksel + 1) * BLOCK
    wide = kvh * HD
    columns = out_weight.shape[1] // n_head
    packet = rows + 8 * max(1, rows // 128)
    bf16, f32 = jnp.bfloat16, jnp.float32
    slots = jax.ShapeDtypeStruct((MOST_BLOCKS * BLOCK, wide), bf16)
    dma = pltpu.SemaphoreType.DMA
    return pl.pallas_call(
        functools.partial(
            layer_kernel, n_ctx, n_head, (samples, group, per, 512), (qblk, kvh, group, ksel, 4)
        ),
        out_shape=(
            jax.ShapeDtypeStruct(span_query.shape, bf16),
            jax.ShapeDtypeStruct((samples, out_weight.shape[1]), bf16),
            slots,
            slots,
        ),
        in_specs=[SM, SM] + [VM] * 5 + [ANY] * 6,
        out_specs=(VM,) * 4,
        scratch_shapes=[
            pltpu.VMEM(cache_key.shape, bf16),
            pltpu.VMEM(cache_value.shape, bf16),
            pltpu.VMEM(span_query.shape, bf16),
            pltpu.VMEM(out_weight.shape, bf16),
            pltpu.VMEM((block_lists.shape[0], BLOCK, wide), bf16),
            pltpu.VMEM((block_lists.shape[0], BLOCK, wide), bf16),
            pltpu.VMEM((rows, resident), f32),
            pltpu.VMEM((width, wide), bf16),
            pltpu.VMEM((width, wide), bf16),
            pltpu.VMEM((n_ctx, packet, HD), f32),
            pltpu.VMEM((n_ctx, packet, HD), f32),
            pltpu.VMEM((n_ctx, samples, per * HD), bf16),
            pltpu.VMEM((n_head, samples, columns), f32),
            pltpu.VMEM((n_head, samples, columns), f32),
            pltpu.VMEM((n_head, samples, columns), bf16),
            dma((6,)),
            dma((2, n_ctx)),
            dma((2, n_ctx)),
            dma((n_ctx,)),
            dma((n_ctx,)),
            dma((n_ctx,)),
            dma((n_ctx,)),
            dma((n_head,)),
            dma((n_head,)),
            dma((n_head,)),
            dma((n_head,)),
        ],
        compiler_params=pltpu.CompilerParams(
            vmem_limit_bytes=62 << 20, collective_id=0, has_side_effects=True
        ),
        name="layer",
    )(
        block_lists,
        owners,
        sample_query,
        span_key,
        span_value,
        sample_key,
        sample_value,
        span_key.reshape(qblk, BLOCK, wide),
        span_value.reshape(qblk, BLOCK, wide),
        cache_key,
        cache_value,
        span_query,
        out_weight,
    )


def solution(mesh):
    c = P("ctx", "head")
    return jax.shard_map(
        functools.partial(local, mesh.shape["ctx"], mesh.shape["head"]),
        mesh=mesh,
        in_specs=(c, c, c, P(), P(), c, c, P(None, "head"), P(None, "head"), P(None, "head"), P("head", "ctx")),
        out_specs=(c, P(None, "ctx"), c, c),
        check_vma=False,
    )
```
